32 devices in a mesh: node: 16 (over z, y, core), chip: 2 (over x).
Axes of the slice: x: 2, y: 2, z: 4, core: 2. Of those that a mesh axis runs over, the one named last changes fastest.
Arguments:
- tokens: bfloat16 [256, 3584], P(('node', 'chip')), may hold values from -6 to 6
- expert_ids: int32 [256, 8], P(('node', 'chip')), may hold values from 0 to 31, as said below
- gate_values: bfloat16 [256, 8], P(('node', 'chip')), may hold values from 0.099609375 to 1
- slot_ids: int32 [256, 8], P(('node', 'chip')), may hold values from 0 to 7, as said below
- up_weight: bfloat16 [32, 3584, 1024], P('node', None, 'chip'), may hold values from -0.09375 to 0.09375
- down_weight: bfloat16 [32, 1024, 3584], P('node', 'chip'), may hold values from -0.1875 to 0.1875
Outputs:
- mixed: bfloat16 [256, 3584], P(('node', 'chip'))
The draws below stay inside these ranges and needn't reach their ends.
Inputs may be any that keep to these rules, and one draw needn't show every extreme that they name: `expert_ids`: each token's 8 entries name, in some order, all 2 experts of each of 4 distinct nodes. `slot_ids`: entries of one token that name experts of the same node hold the same slot; among the 16 tokens of one node (aligned blocks of the token dimension), the slots to one destination node are distinct, and some destination node receives all 8 slots from each source node.
All inputs are finite; a program needn't handle non-finite values.
Results may differ from the reference program's by a relative error of at most 0.0058.
Values may be sent and summed in bfloat16 or wider, within the bound.
A program may use at most 64 MiB of HBM per device.

```python
import math
import jax
import jax.numpy as jnp
from jax import lax

D = 3584
FF = 1024
EXP_NODE = 2
TOPK = 8
TOPN = 4
TOK_NODE = 16
TOKENS = 256
EXPERTS = 32
CAP_N = 8
N_NODE = 16
N_CHIP = 2


def route_block(key):
    key_count, key_node, key_token, key_order = jax.random.split(key, 4)
    pairs = N_NODE // 2
    shares = jax.random.randint(key_count, (pairs,), 0, CAP_N + 1, dtype=jnp.int32)
    shares = shares.at[0].set(CAP_N)
    counts = jnp.stack([shares, CAP_N - shares], axis=1).reshape(N_NODE)
    ends = jnp.cumsum(counts).astype(jnp.int32)
    starts = ends - counts
    entry = jnp.arange(TOPN * TOK_NODE, dtype=jnp.int32)
    group = jnp.sum((entry[:, None] >= ends[None, :]).astype(jnp.int32), axis=1)
    slot = entry - starts[group]
    token = entry % TOK_NODE
    column = entry // TOK_NODE
    labels = jax.random.permutation(key_node, N_NODE).astype(jnp.int32)
    node = labels[group]
    token_perm = jax.random.permutation(key_token, TOK_NODE).astype(jnp.int32)
    owner = token_perm[token]
    node_grid = jnp.zeros((TOK_NODE, TOPN), jnp.int32).at[owner, column].set(node)
    slot_grid = jnp.zeros((TOK_NODE, TOPN), jnp.int32).at[owner, column].set(slot)
    local = jnp.arange(EXP_NODE, dtype=jnp.int32)
    ids_full = (node_grid[:, :, None] * EXP_NODE + local[None, None, :]).reshape(TOK_NODE, TOPK)
    slots_full = jnp.broadcast_to(slot_grid[:, :, None], (TOK_NODE, TOPN, EXP_NODE)).reshape(TOK_NODE, TOPK)
    scores = jax.random.randint(key_order, (TOK_NODE, TOPK), 0, 1 << 20, dtype=jnp.int32) * TOPK + jnp.arange(TOPK, dtype=jnp.int32)[None, :]
    order = jnp.argsort(scores, axis=1, stable=True).astype(jnp.int32)
    return (jnp.take_along_axis(ids_full, order, axis=1), jnp.take_along_axis(slots_full, order, axis=1))


def route_all(key):
    base = jax.random.fold_in(key, 7331)
    node_keys = jax.vmap(lambda index: jax.random.fold_in(base, index))(jnp.arange(N_NODE, dtype=jnp.int32))
    ids_all, slots_all = jax.vmap(route_block)(node_keys)
    return (ids_all.reshape(TOKENS, TOPK), slots_all.reshape(TOKENS, TOPK))


def draw_expert_ids(key, part):
    return route_all(key)[0]


def draw_slot_ids(key, part):
    return route_all(key)[1]


def block_scale(key, extent, shards, low, high):
    factor_of = 1.0
    for dim, parts in shards:
        heights = jax.random.uniform(jax.random.fold_in(jax.random.fold_in(key, 6), dim), (parts,), jnp.float32, low / len(shards), high / len(shards))
        factor_of = factor_of * jnp.repeat(jnp.exp(heights), extent[dim] // parts).reshape((-1,) + (1,) * (len(extent) - 1 - dim))
    return factor_of


def noise(stream_key, dims, width, bound, pieces=(), held_as=jnp.bfloat16):
    level = block_scale(stream_key, dims, pieces, -0.22, 0.18) if pieces else 1.0
    values = jax.random.normal(stream_key, dims, jnp.float32) * width * level
    return jnp.minimum(jnp.maximum(values, -bound), bound).astype(held_as)


def setup_inputs(seed: int = 0) -> dict:
    key_of = jax.random.split(jax.random.key(seed), 7)
    return {
        "tokens": noise(key_of[0], (TOKENS, D), 1.0, 6.0, ((0, 32),)),
        "expert_ids": draw_expert_ids(jax.random.fold_in(key_of[6], 71), 0),
        "gate_values": jnp.clip(jnp.exp(math.log(1.0) - 2.306499 * jax.random.uniform(key_of[2], (TOKENS, TOPK), jnp.float32) ** block_scale(key_of[2], (TOKENS, TOPK), ((0, 32),), -0.2, 0.2)), 0.099609375, 1.0).astype(jnp.bfloat16),
        "slot_ids": draw_slot_ids(jax.random.fold_in(key_of[6], 71), 0),
        "up_weight": noise(key_of[4], (EXPERTS, D, FF), D ** -0.5, 0.09375, ((0, 16), (2, 2))),
        "down_weight": noise(key_of[5], (EXPERTS, FF, D), FF ** -0.5, 0.1875, ((0, 16), (1, 2))),
    }


def reference(tokens, expert_ids, gate_values, slot_ids, up_weight, down_weight):
    rows_node = N_NODE * CAP_N
    block_width = FF // N_CHIP
    token_index = jnp.arange(TOKENS, dtype=jnp.int32)
    source_node = token_index // TOK_NODE
    flat_rows = (expert_ids // EXP_NODE) * rows_node + source_node[:, None] * CAP_N + slot_ids
    flat_rows = flat_rows.astype(jnp.int32).reshape(-1)
    owner_ids = jnp.broadcast_to(token_index[:, None], expert_ids.shape).reshape(-1)
    owners = jnp.full((N_NODE * rows_node,), TOKENS, jnp.int32).at[flat_rows].set(owner_ids)
    local_ids = (expert_ids % EXP_NODE).astype(jnp.int32).reshape(-1)
    gate_table = jnp.zeros((N_NODE * rows_node, EXP_NODE), jnp.float32)
    gate_table = gate_table.at[flat_rows, local_ids].set(gate_values.astype(jnp.float32).reshape(-1))
    padded = jnp.concatenate([tokens, jnp.zeros((1, D), tokens.dtype)], axis=0)
    owners = owners.reshape(N_NODE, rows_node)
    gate_table = gate_table.reshape(N_NODE, rows_node, EXP_NODE)
    up_nodes = up_weight.reshape(N_NODE, EXP_NODE, D, FF)
    down_nodes = down_weight.reshape(N_NODE, EXP_NODE, FF, D)

    def serve(totals, inputs):
        node_owners, node_gates, up_node, down_node = inputs
        routed = padded[node_owners]
        result = jnp.zeros((rows_node, N_CHIP, D), jnp.float32)
        for expert in range(EXP_NODE):
            hidden = jax.nn.silu(jnp.dot(routed, up_node[expert], preferred_element_type=jnp.float32)).astype(jnp.bfloat16)
            blocks = hidden.reshape(rows_node, N_CHIP, block_width).astype(jnp.float32)
            down_blocks = down_node[expert].reshape(N_CHIP, block_width, D).astype(jnp.float32)
            result = result + node_gates[:, expert][:, None, None] * jnp.einsum("rcf,cfd->rcd", blocks, down_blocks)
        rounded = lax.optimization_barrier(result.astype(jnp.bfloat16))
        served = jnp.sum(rounded.astype(jnp.float32), axis=1)
        return totals.at[node_owners].add(served), None

    totals = jnp.zeros((TOKENS + 1, D), jnp.float32)
    totals, unused = lax.scan(serve, totals, (owners, gate_table, up_nodes, down_nodes))
    return totals[:TOKENS].astype(jnp.bfloat16)
```

```python
import functools

import jax
import jax.numpy as jnp
from jax import lax
from jax.experimental import pallas as pl
from jax.experimental.pallas import tpu as pltpu
from jax.sharding import PartitionSpec as P


def pack_rows(targets, experts, node_tokens, node_gates, row_count, per_node):
    row_ids = jnp.arange(row_count, dtype=jnp.int32)
    matches = (targets[None, :, :] == row_ids[:, None, None]).astype(jnp.bfloat16)
    picked = jnp.minimum(jnp.sum(matches.astype(jnp.float32), axis=2), 1.0).astype(jnp.bfloat16)
    packed = jnp.dot(picked, node_tokens, preferred_element_type=jnp.float32).astype(jnp.bfloat16)
    choose = (experts[:, :, None] == jnp.arange(per_node, dtype=jnp.int32)[None, None, :]).astype(
        jnp.bfloat16
    )
    weighted = choose * node_gates[:, :, None]
    gate_rows = jnp.einsum(
        "rtk,tke->re", matches, weighted, preferred_element_type=jnp.float32
    ).astype(jnp.bfloat16)
    return (packed, gate_rows)


def expert_rows(row_block, gate_block, up_local, down_local):
    result = jnp.zeros((row_block.shape[0], down_local.shape[2]), jnp.float32)
    for expert in range(up_local.shape[0]):
        hidden = jax.nn.silu(
            jnp.dot(row_block, up_local[expert], preferred_element_type=jnp.float32)
        ).astype(jnp.bfloat16)
        product = jnp.dot(hidden, down_local[expert], preferred_element_type=jnp.float32)
        result = result + gate_block[:, expert : expert + 1].astype(jnp.float32) * product
    return result.astype(jnp.bfloat16)


def gather_sum(indices, table):
    valid = indices >= 0
    safe = jnp.where(valid, indices, 0).reshape(-1)
    picked = jnp.take(table, safe, axis=0).reshape(
        indices.shape[0], indices.shape[1], table.shape[1]
    )
    return jnp.sum(jnp.where(valid[:, :, None], picked, 0.0), axis=1)


def shards(tokens, expert_ids, gate_values, slot_ids, up_weight, down_weight):
    node_count = lax.axis_size("node")
    chip_count = lax.axis_size("chip")
    my_chip = lax.axis_index("chip")
    tok_dev = tokens.shape[0]
    model_dim = tokens.shape[1]
    per_node = up_weight.shape[0]
    capacity = 8 * chip_count * tok_dev // node_count
    block_cap = capacity // chip_count
    route_code = (expert_ids // per_node * capacity + slot_ids) * per_node + expert_ids % per_node
    node_tokens, node_gates = (
        lax.all_gather(tokens, "chip", axis=0, tiled=True),
        lax.all_gather(gate_values, "chip", axis=0, tiled=True),
    )
    node_codes = lax.all_gather(route_code, "chip", axis=0, tiled=True)
    node_expert = node_codes % per_node
    node_slot = node_codes // per_node % capacity
    node_dest = node_codes // per_node // capacity
    targets = node_dest * capacity + node_slot
    packed, gate_rows = pack_rows(
        targets, node_expert, node_tokens, node_gates, node_count * capacity, per_node
    )
    shaped = packed.reshape(node_count, chip_count, 1, block_cap, model_dim)
    gate_shaped = gate_rows.reshape(node_count, chip_count, 1, block_cap, per_node)
    arrived, arrived_gates = (
        lax.all_to_all(shaped, "node", split_axis=0, concat_axis=2, tiled=True),
        lax.all_to_all(gate_shaped, "node", split_axis=0, concat_axis=2, tiled=True),
    )
    row_block = arrived.reshape(-1, model_dim)
    gate_block = arrived_gates.reshape(-1, per_node)
    partial_value = expert_rows(row_block, gate_block, up_weight, down_weight)
    pieces = lax.all_to_all(
        partial_value.reshape(chip_count, node_count * block_cap, model_dim),
        "chip",
        split_axis=0,
        concat_axis=0,
        tiled=True,
    )
    slot_sums = jnp.sum(pieces.astype(jnp.float32), axis=0).reshape(
        node_count, block_cap, model_dim
    )
    held = lax.all_to_all(slot_sums, "node", split_axis=0, concat_axis=0, tiled=True).reshape(
        node_count * block_cap, model_dim
    )
    wanted = (node_slot // block_cap == my_chip) & (node_expert == 0)
    indices = jnp.where(wanted, node_dest * block_cap + node_slot % block_cap, -1)
    term = gather_sum(indices, held)
    summed = lax.psum_scatter(term, "chip", scatter_dimension=0, tiled=True)
    return summed.astype(jnp.bfloat16)


LANES = 128
PIECES = 4
MESH = pl.DeviceIdType.MESH


def fused_kernel(
    nz, tokens_ref, ids_ref, gates_ref, up_hbm, down_hbm, out_ref,
    up_v, down_v, gath, rows_v, hid_v, total,
    core_out, core_in, one_out, one_in, two_out, two_in, z_out, z_in,
    local_sem, up_sem, down_sem,
    gz_send, gz_recv, g1_send, g1_recv, g2_send, g2_recv, gc_send, gc_recv,
    r_send, r_recv,
):
    f32, bf16 = jnp.float32, jnp.bfloat16
    node, x = lax.axis_index("node"), lax.axis_index("chip")
    c = lax.rem(node, 2)
    y = lax.rem(lax.div(node, 2), 2)
    z = lax.div(node, 4)
    model = tokens_ref.shape[1]
    per_node = up_v.shape[0]
    half = model // 2
    piece = model // PIECES
    blocks = 8 * nz
    per_core = 4 * nz

    def dev(zz, yy, cc, xx):
        return ((zz * 2 + yy) * 2 + cc, xx)

    def block(cc, xx, yy, zz):
        return ((cc * 2 + xx) * 2 + yy) * nz + zz

    def z_peer(j):
        return dev(lax.rem(z + j, nz), y, c, x)

    x_peer, y_peer, c_peer = dev(z, y, c, 1 - x), dev(z, 1 - y, c, x), dev(z, y, 1 - c, x)

    own = block(c, x, y, z)
    stage = pltpu.make_async_copy(tokens_ref, gath.at[own, :, pl.ds(0, model)], local_sem)
    stage.start()
    up_copies = []
    down_copies = []
    for e in range(per_node):
        up_copies.append(pltpu.make_async_copy(up_hbm.at[e], up_v.at[e], up_sem.at[e]))
        down_copies.append(pltpu.make_async_copy(down_hbm.at[e], down_v.at[e], down_sem.at[e]))

    lanes = lax.broadcasted_iota(jnp.int32, (tokens_ref.shape[0], LANES), 1)
    table = jnp.zeros((tokens_ref.shape[0], LANES), f32)
    ids = ids_ref[...]
    gates = gates_ref[...].astype(f32)
    for k in range(ids.shape[1]):
        table = table + jnp.where(ids[:, k : k + 1] == lanes, gates[:, k : k + 1], 0.0)
    gath[own, :, pl.ds(model, LANES)] = table.astype(bf16)

    barrier = pltpu.get_barrier_semaphore()
    peers = [z_peer(j) for j in range(1, nz)] + [y_peer, x_peer, c_peer]
    for peer in peers:
        pl.semaphore_signal(barrier, inc=1, device_id=peer, device_id_type=MESH)
    stage.wait()
    pl.semaphore_wait(barrier, len(peers))

    spans = [pl.ds(0, half), pl.ds(half, half + LANES)]
    sends = []

    def send(src, dst, ssem, rsem, peer):
        copy = pltpu.make_async_remote_copy(
            src_ref=src, dst_ref=dst, send_sem=ssem, recv_sem=rsem,
            device_id=peer, device_id_type=MESH,
        )
        copy.start()
        sends.append(copy)
        return copy

    def gsend(h, b, ssem, rsem, peer):
        ref = gath.at[b, :, spans[h]]
        return send(ref, ref, ssem, rsem, peer)

    firsts = [y_peer, x_peer]
    seconds = [x_peer, y_peer]

    def mine(h, k):
        return block(c, x, y, lax.rem(z + nz - k, nz))

    def other(h, k):
        zz = lax.rem(z + nz - k, nz)
        return block(c, x, 1 - y, zz) if h == 0 else block(c, 1 - x, y, zz)

    zc = {}
    first = {}
    second = {}
    for h in range(2):
        for j in range(1, nz):
            zc[h, j] = gsend(h, own, gz_send.at[h, j - 1], gz_recv.at[h, j - 1], z_peer(j))

    def forward_mine(h, k):
        if k:
            zc[h, k].wait_recv()
        first[h, k] = gsend(h, mine(h, k), g1_send.at[h, k], g1_recv.at[h, k], firsts[h])
        second[h, k] = gsend(h, mine(h, k), g2_send.at[h, k], g2_recv.at[h, k], seconds[h])

    def forward_other(h, k):
        first[h, k].wait_recv()
        second[h, nz + k] = gsend(
            h, other(h, k), g2_send.at[h, nz + k], g2_recv.at[h, nz + k], seconds[h]
        )

    corec = {}

    def share(h, g, xx, yy):
        ref = gath.at[pl.ds(block(c, xx, yy, 0), nz), :, spans[h]]
        corec[h, g] = send(ref, ref, gc_send.at[h, g], gc_recv.at[h, g], c_peer)

    forward_mine(0, 0)
    forward_mine(1, 0)
    for copy in up_copies + down_copies:
        copy.start()
    for k in range(1, nz):
        for h in range(2):
            forward_mine(h, k)
        for h in range(2):
            forward_other(h, k - 1)
    for h in range(2):
        share(h, 0, x, y)
    for h in range(2):
        forward_other(h, nz - 1)
    share(0, 1, x, 1 - y)
    share(1, 1, 1 - x, y)
    for g in range(2):
        for h in range(2):
            for k in range(nz):
                second[h, g * nz + k].wait_recv()
        if g == 0:
            share(0, 2, 1 - x, y)
            share(1, 2, x, 1 - y)
        else:
            share(0, 3, 1 - x, 1 - y)
            share(1, 3, 1 - x, 1 - y)
    for copy in corec.values():
        copy.wait_recv()
    for copy in sends:
        copy.wait_send()

    def pack(i, carry):
        pair = gath[pl.ds(2 * i, 2), :, pl.ds(0, model)].astype(f32)
        flat = pair.reshape(2 * pair.shape[1], model).astype(bf16)
        rows_v[pl.ds(pl.multiple_of(16 * i, 16), 16), :] = flat
        return carry

    lax.fori_loop(0, blocks // 2, pack, 0)
    table = gath[:, :, pl.ds(model, LANES)].astype(f32).reshape(rows_v.shape[0], LANES)
    lane = lax.broadcasted_iota(jnp.int32, table.shape, 1)
    weight = [
        jnp.sum(jnp.where(lane == node * per_node + e, table, 0.0), axis=1, keepdims=True)
        for e in range(per_node)
    ]

    for copy in up_copies:
        copy.wait()

    def up_step(e, carry):
        value = jnp.dot(rows_v[...], up_v[e], preferred_element_type=f32)
        hid_v[e] = (value / (1.0 + jnp.exp(-value))).astype(bf16)
        return carry

    lax.fori_loop(0, per_node, up_step, 0)
    for copy in down_copies:
        copy.wait()

    rsends = []
    corer, oner, twor, zr = {}, {}, {}, {}

    def rsend(src, dst, q, s, peer):
        copy = pltpu.make_async_remote_copy(
            src_ref=src, dst_ref=dst, send_sem=r_send.at[q, s], recv_sem=r_recv.at[q, s],
            device_id=peer, device_id_type=MESH,
        )
        copy.start()
        rsends.append(copy)
        return copy

    def produce(q):
        cols = pl.ds(q * piece, piece)
        value = weight[0] * jnp.dot(hid_v[0], down_v[0, :, cols], preferred_element_type=f32)
        for e in range(1, per_node):
            value = value + weight[e] * jnp.dot(
                hid_v[e], down_v[e, :, cols], preferred_element_type=f32
            )
        total[q] = value.reshape(blocks, rows_v.shape[0] // blocks, piece)
        core_out[q] = total[q, pl.ds((1 - c) * per_core, per_core)].astype(bf16)
        corer[q] = rsend(core_out.at[q], core_in.at[q], q, 0, c_peer)

    def after_core(q):
        corer[q].wait_recv()
        base = c * per_core
        if q % 2 == 0:
            far = pl.ds(base + (1 - x) * 2 * nz, 2 * nz)
            near = pl.ds(base + x * 2 * nz, 2 * nz)
            one_out[q] = (
                total[q, far] + core_in[q, pl.ds((1 - x) * 2 * nz, 2 * nz)].astype(f32)
            ).astype(bf16)
            oner[q] = rsend(one_out.at[q], one_in.at[q], q, 1, x_peer)
            total[q, near] += core_in[q, pl.ds(x * 2 * nz, 2 * nz)].astype(f32)
        else:
            for xx in range(2):
                off = xx * 2 * nz + (1 - y) * nz
                one_out[q, xx * nz : (xx + 1) * nz] = (
                    total[q, pl.ds(base + off, nz)] + core_in[q, pl.ds(off, nz)].astype(f32)
                ).astype(bf16)
            oner[q] = rsend(one_out.at[q], one_in.at[q], q, 1, y_peer)
            for xx in range(2):
                off = xx * 2 * nz + y * nz
                total[q, pl.ds(base + off, nz)] += core_in[q, pl.ds(off, nz)].astype(f32)

    def after_one(q):
        oner[q].wait_recv()
        near = pl.ds(block(c, x, y, 0), nz)
        if q % 2 == 0:
            far, slot_far, slot_near, peer = block(c, x, 1 - y, 0), 1 - y, y, y_peer
        else:
            far, slot_far, slot_near, peer = block(c, 1 - x, y, 0), 1 - x, x, x_peer
        two_out[q] = (
            total[q, pl.ds(far, nz)] + one_in[q, pl.ds(slot_far * nz, nz)].astype(f32)
        ).astype(bf16)
        twor[q] = rsend(two_out.at[q], two_in.at[q], q, 2, peer)
        total[q, near] += one_in[q, pl.ds(slot_near * nz, nz)].astype(f32)

    def after_two(q):
        twor[q].wait_recv()
        base = block(c, x, y, 0)
        for j in range(1, nz):
            zz = lax.rem(z + j, nz)
            z_out[q, j - 1] = (total[q, base + zz] + two_in[q, zz].astype(f32)).astype(bf16)
            zr[q, j] = rsend(
                z_out.at[q, j - 1], z_in.at[q, j - 1], q, 2 + j, z_peer(j)
            )
        total[q, base + z] += two_in[q, z].astype(f32)

    def finish(q):
        value = total[q, own]
        for j in range(1, nz):
            zr[q, j].wait_recv()
            value = value + z_in[q, j - 1].astype(f32)
        out_ref[:, pl.ds(q * piece, piece)] = value.astype(out_ref.dtype)

    steps = [produce, after_core, after_one, after_two, finish]
    for t in range(PIECES + len(steps) - 1):
        for s, step in enumerate(steps):
            if 0 <= t - s < PIECES:
                step(t - s)
    for copy in rsends:
        copy.wait_send()


def fused(nz, tokens, expert_ids, gate_values, slot_ids, up_weight, down_weight):
    tok, model = tokens.shape
    per_node, _, width = up_weight.shape
    blocks = 8 * nz
    piece = model // PIECES
    bf16, f32 = jnp.bfloat16, jnp.float32
    vmem = pl.BlockSpec(memory_space=pltpu.VMEM)
    anyspace = pl.BlockSpec(memory_space=pl.ANY)
    dma = pltpu.SemaphoreType.DMA

    def pieces(n):
        return pltpu.VMEM((PIECES, n, tok, piece), bf16)

    return pl.pallas_call(
        functools.partial(fused_kernel, nz),
        out_shape=jax.ShapeDtypeStruct((tok, model), bf16),
        in_specs=[anyspace, vmem, vmem, anyspace, anyspace],
        out_specs=vmem,
        scratch_shapes=[
            pltpu.VMEM(up_weight.shape, bf16),
            pltpu.VMEM(down_weight.shape, bf16),
            pltpu.VMEM((blocks, tok, model + LANES), bf16),
            pltpu.VMEM((blocks * tok, model), bf16),
            pltpu.VMEM((per_node, blocks * tok, width), bf16),
            pltpu.VMEM((PIECES, blocks, tok, piece), f32),
            pieces(4 * nz), pieces(4 * nz),
            pieces(2 * nz), pieces(2 * nz),
            pieces(nz), pieces(nz),
            pieces(nz - 1), pieces(nz - 1),
            dma, dma((per_node,)), dma((per_node,)),
            dma((2, nz - 1)), dma((2, nz - 1)),
            dma((2, nz)), dma((2, nz)),
            dma((2, 2 * nz)), dma((2, 2 * nz)),
            dma((2, 4)), dma((2, 4)),
            dma((PIECES, 2 + nz)), dma((PIECES, 2 + nz)),
        ],
        compiler_params=pltpu.CompilerParams(
            collective_id=0, has_side_effects=True, vmem_limit_bytes=60 * 1024 * 1024
        ),
    )(tokens, expert_ids, gate_values, up_weight, down_weight)


def body_for(mesh):
    nodes, chips = mesh.shape["node"], mesh.shape["chip"]
    nz = nodes // 4

    def body(tokens, expert_ids, gate_values, slot_ids, up_weight, down_weight):
        tok, model = tokens.shape
        experts = nodes * up_weight.shape[0]
        if (
            chips == 2
            and nodes == 4 * nz
            and 2 <= nz <= 4
            and tok == 8
            and model % (PIECES * LANES) == 0
            and experts <= LANES
        ):
            return fused(nz, tokens, expert_ids, gate_values, slot_ids, up_weight, down_weight)
        return shards(tokens, expert_ids, gate_values, slot_ids, up_weight, down_weight)

    return body


def solution(mesh):
    return jax.shard_map(
        body_for(mesh),
        mesh=mesh,
        in_specs=(
            P(("node", "chip"), None),
            P(("node", "chip"), None),
            P(("node", "chip"), None),
            P(("node", "chip"), None),
            P("node", None, "chip"),
            P("node", "chip", None),
        ),
        out_specs=P(("node", "chip"), None),
        check_vma=False,
    )
```

```python
import functools

import jax
import jax.numpy as jnp
from jax import lax
from jax.experimental import pallas as pl
from jax.experimental.pallas import tpu as pltpu
from jax.sharding import PartitionSpec as P


def pack_rows(targets, experts, node_tokens, node_gates, row_count, per_node):
    row_ids = jnp.arange(row_count, dtype=jnp.int32)
    matches = (targets[None, :, :] == row_ids[:, None, None]).astype(jnp.bfloat16)
    picked = jnp.minimum(jnp.sum(matches.astype(jnp.float32), axis=2), 1.0).astype(jnp.bfloat16)
    packed = jnp.dot(picked, node_tokens, preferred_element_type=jnp.float32).astype(jnp.bfloat16)
    choose = (experts[:, :, None] == jnp.arange(per_node, dtype=jnp.int32)[None, None, :]).astype(
        jnp.bfloat16
    )
    weighted = choose * node_gates[:, :, None]
    gate_rows = jnp.einsum(
        "rtk,tke->re", matches, weighted, preferred_element_type=jnp.float32
    ).astype(jnp.bfloat16)
    return (packed, gate_rows)


def expert_rows(row_block, gate_block, up_local, down_local):
    result = jnp.zeros((row_block.shape[0], down_local.shape[2]), jnp.float32)
    for expert in range(up_local.shape[0]):
        hidden = jax.nn.silu(
            jnp.dot(row_block, up_local[expert], preferred_element_type=jnp.float32)
        ).astype(jnp.bfloat16)
        product = jnp.dot(hidden, down_local[expert], preferred_element_type=jnp.float32)
        result = result + gate_block[:, expert : expert + 1].astype(jnp.float32) * product
    return result.astype(jnp.bfloat16)


def gather_sum(indices, table):
    valid = indices >= 0
    safe = jnp.where(valid, indices, 0).reshape(-1)
    picked = jnp.take(table, safe, axis=0).reshape(
        indices.shape[0], indices.shape[1], table.shape[1]
    )
    return jnp.sum(jnp.where(valid[:, :, None], picked, 0.0), axis=1)


def shards(tokens, expert_ids, gate_values, slot_ids, up_weight, down_weight):
    node_count = lax.axis_size("node")
    chip_count = lax.axis_size("chip")
    my_chip = lax.axis_index("chip")
    tok_dev = tokens.shape[0]
    model_dim = tokens.shape[1]
    per_node = up_weight.shape[0]
    capacity = 8 * chip_count * tok_dev // node_count
    block_cap = capacity // chip_count
    route_code = (expert_ids // per_node * capacity + slot_ids) * per_node + expert_ids % per_node
    node_tokens, node_gates = (
        lax.all_gather(tokens, "chip", axis=0, tiled=True),
        lax.all_gather(gate_values, "chip", axis=0, tiled=True),
    )
    node_codes = lax.all_gather(route_code, "chip", axis=0, tiled=True)
    node_expert = node_codes % per_node
    node_slot = node_codes // per_node % capacity
    node_dest = node_codes // per_node // capacity
    targets = node_dest * capacity + node_slot
    packed, gate_rows = pack_rows(
        targets, node_expert, node_tokens, node_gates, node_count * capacity, per_node
    )
    shaped = packed.reshape(node_count, chip_count, 1, block_cap, model_dim)
    gate_shaped = gate_rows.reshape(node_count, chip_count, 1, block_cap, per_node)
    arrived, arrived_gates = (
        lax.all_to_all(shaped, "node", split_axis=0, concat_axis=2, tiled=True),
        lax.all_to_all(gate_shaped, "node", split_axis=0, concat_axis=2, tiled=True),
    )
    row_block = arrived.reshape(-1, model_dim)
    gate_block = arrived_gates.reshape(-1, per_node)
    partial_value = expert_rows(row_block, gate_block, up_weight, down_weight)
    pieces = lax.all_to_all(
        partial_value.reshape(chip_count, node_count * block_cap, model_dim),
        "chip",
        split_axis=0,
        concat_axis=0,
        tiled=True,
    )
    slot_sums = jnp.sum(pieces.astype(jnp.float32), axis=0).reshape(
        node_count, block_cap, model_dim
    )
    held = lax.all_to_all(slot_sums, "node", split_axis=0, concat_axis=0, tiled=True).reshape(
        node_count * block_cap, model_dim
    )
    wanted = (node_slot // block_cap == my_chip) & (node_expert == 0)
    indices = jnp.where(wanted, node_dest * block_cap + node_slot % block_cap, -1)
    term = gather_sum(indices, held)
    summed = lax.psum_scatter(term, "chip", scatter_dimension=0, tiled=True)
    return summed.astype(jnp.bfloat16)


LANES = 128
PIECES = 4
MESH = pl.DeviceIdType.MESH


def fused_kernel(
    nz, tokens_ref, ids_ref, gates_ref, up_hbm, down_hbm, out_ref,
    up_v, down_v, gath, rows_v, hid_v, total,
    core_out, core_in, plane_out, plane_in, z_out, z_in,
    local_sem, up_sem, down_sem,
    gz_send, gz_recv, ge_send, ge_recv, gp_send, gp_recv, gf_send, gf_recv, gc_send, gc_recv,
    r_send, r_recv,
):
    f32, bf16 = jnp.float32, jnp.bfloat16
    node, x = lax.axis_index("node"), lax.axis_index("chip")
    c = lax.rem(node, 2)
    y = lax.rem(lax.div(node, 2), 2)
    z = lax.div(node, 4)
    model = tokens_ref.shape[1]
    per_node = up_v.shape[0]
    piece = model // PIECES
    blocks = 8 * nz
    per_core = 4 * nz

    def dev(zz, yy, cc, xx):
        return ((zz * 2 + yy) * 2 + cc, xx)

    def block(cc, xx, yy, zz):
        return ((cc * 2 + xx) * 2 + yy) * nz + zz

    def z_peer(j):
        return dev(lax.rem(z + j, nz), y, c, x)

    c_peer = dev(z, y, 1 - c, x)
    plane_at = [(1 - x, 1 - y), (1 - x, y), (x, 1 - y)]
    plane_peers = [dev(z, yy, c, xx) for xx, yy in plane_at]

    own = block(c, x, y, z)
    stage = pltpu.make_async_copy(tokens_ref, gath.at[own, :, pl.ds(0, model)], local_sem)
    stage.start()
    up_copies = []
    down_copies = []
    for e in range(per_node):
        up_copies.append(pltpu.make_async_copy(up_hbm.at[e], up_v.at[e], up_sem.at[e]))
        down_copies.append(pltpu.make_async_copy(down_hbm.at[e], down_v.at[e], down_sem.at[e]))

    lanes = lax.broadcasted_iota(jnp.int32, (tokens_ref.shape[0], LANES), 1)
    table = jnp.zeros((tokens_ref.shape[0], LANES), f32)
    ids = ids_ref[...]
    gates = gates_ref[...].astype(f32)
    for k in range(ids.shape[1]):
        table = table + jnp.where(ids[:, k : k + 1] == lanes, gates[:, k : k + 1], 0.0)
    gath[own, :, pl.ds(model, LANES)] = table.astype(bf16)

    barrier = pltpu.get_barrier_semaphore()
    peers = [z_peer(j) for j in range(1, nz)] + plane_peers + [c_peer]
    for peer in peers:
        pl.semaphore_signal(barrier, inc=1, device_id=peer, device_id_type=MESH)
    stage.wait()
    pl.semaphore_wait(barrier, len(peers))

    sends = []

    def send(src, dst, ssem, rsem, peer):
        copy = pltpu.make_async_remote_copy(
            src_ref=src, dst_ref=dst, send_sem=ssem, recv_sem=rsem,
            device_id=peer, device_id_type=MESH,
        )
        copy.start()
        sends.append(copy)
        return copy

    early = pl.ds(0, piece)
    late = pl.ds(piece, model + LANES - piece)

    def gsend(ref, ssem, rsem, peer):
        return send(ref, ref, ssem, rsem, peer)

    def behind(k):
        return lax.rem(z + nz - k, nz)

    zc, plane, ec, ez, shared = {}, {}, {}, {}, []
    for j in range(1, nz):
        zc[j] = gsend(gath.at[own, :, late], gz_send.at[j - 1], gz_recv.at[j - 1], z_peer(j))
    for p in range(3):
        ec[p] = gsend(gath.at[own, :, early], ge_send.at[p], ge_recv.at[p], plane_peers[p])

    def forward_late(k):
        if k:
            zc[k].wait_recv()
        ref = gath.at[block(c, x, y, behind(k)), :, late]
        for p in range(3):
            plane[p, k] = gsend(ref, gp_send.at[p, k], gp_recv.at[p, k], plane_peers[p])

    def forward_early(g):
        if g:
            ec[g - 1].wait_recv()
        xx, yy = plane_at[g - 1] if g else (x, y)
        ref = gath.at[block(c, xx, yy, z), :, early]
        for j in range(1, nz):
            ez[g, j] = gsend(ref, gf_send.at[g, j - 1], gf_recv.at[g, j - 1], z_peer(j))

    forward_late(0)
    forward_early(0)
    for copy in up_copies + down_copies:
        copy.start()
    for k in range(1, nz):
        forward_late(k)
        if k == 1:
            for g in range(1, 4):
                forward_early(g)
    for g in range(4):
        xx, yy = plane_at[g - 1] if g else (x, y)
        for j in range(1, nz):
            ez[g, j].wait_recv()
        if g:
            for k in range(nz):
                plane[g - 1, k].wait_recv()
        ref = gath.at[pl.ds(block(c, xx, yy, 0), nz)]
        shared.append(gsend(ref, gc_send.at[g], gc_recv.at[g], c_peer))
    for copy in shared:
        copy.wait_recv()
    for copy in sends:
        copy.wait_send()

    def pack(i, carry):
        pair = gath[pl.ds(2 * i, 2), :, pl.ds(0, model)].astype(f32)
        flat = pair.reshape(2 * pair.shape[1], model).astype(bf16)
        rows_v[pl.ds(pl.multiple_of(16 * i, 16), 16), :] = flat
        return carry

    lax.fori_loop(0, blocks // 2, pack, 0)
    table = gath[:, :, pl.ds(model, LANES)].astype(f32).reshape(rows_v.shape[0], LANES)
    lane = lax.broadcasted_iota(jnp.int32, table.shape, 1)
    weight = [
        jnp.sum(jnp.where(lane == node * per_node + e, table, 0.0), axis=1, keepdims=True)
        for e in range(per_node)
    ]

    for copy in up_copies:
        copy.wait()

    def up_step(e, carry):
        value = jnp.dot(rows_v[...], up_v[e], preferred_element_type=f32)
        hid_v[e] = (value / (1.0 + jnp.exp(-value))).astype(bf16)
        return carry

    lax.fori_loop(0, per_node, up_step, 0)
    for copy in down_copies:
        copy.wait()

    rsends = []
    corer, planer, zr = {}, {}, {}

    def rsend(src, dst, q, s, peer):
        copy = pltpu.make_async_remote_copy(
            src_ref=src, dst_ref=dst, send_sem=r_send.at[q, s], recv_sem=r_recv.at[q, s],
            device_id=peer, device_id_type=MESH,
        )
        copy.start()
        rsends.append(copy)
        return copy

    def produce(q):
        cols = pl.ds(q * piece, piece)
        value = weight[0] * jnp.dot(hid_v[0], down_v[0, :, cols], preferred_element_type=f32)
        for e in range(1, per_node):
            value = value + weight[e] * jnp.dot(
                hid_v[e], down_v[e, :, cols], preferred_element_type=f32
            )
        total[q] = value.reshape(blocks, rows_v.shape[0] // blocks, piece)
        core_out[q] = total[q, pl.ds((1 - c) * per_core, per_core)].astype(bf16)
        corer[q] = rsend(core_out.at[q], core_in.at[q], q, 0, c_peer)

    def after_core(q):
        corer[q].wait_recv()
        for p, (xx, yy) in enumerate(plane_at):
            slots = pl.ds(p * nz, nz)
            plane_out[q, slots] = (
                total[q, pl.ds(block(c, xx, yy, 0), nz)]
                + core_in[q, pl.ds(block(0, xx, yy, 0), nz)].astype(f32)
            ).astype(bf16)
            planer[q, p] = rsend(
                plane_out.at[q, slots], plane_in.at[q, slots], q, 1 + p, plane_peers[p]
            )
        near = pl.ds(block(c, x, y, 0), nz)
        total[q, near] += core_in[q, pl.ds(block(0, x, y, 0), nz)].astype(f32)

    def after_plane(q):
        near = pl.ds(block(c, x, y, 0), nz)
        value = total[q, near]
        for p in range(3):
            planer[q, p].wait_recv()
            value = value + plane_in[q, p * nz : (p + 1) * nz].astype(f32)
        total[q, near] = value
        for j in range(1, nz):
            z_out[q, j - 1] = total[q, block(c, x, y, lax.rem(z + j, nz))].astype(bf16)
            zr[q, j] = rsend(
                z_out.at[q, j - 1], z_in.at[q, j - 1], q, 3 + j, z_peer(j)
            )

    def finish(q):
        value = total[q, own]
        for j in range(1, nz):
            zr[q, j].wait_recv()
            value = value + z_in[q, j - 1].astype(f32)
        out_ref[:, pl.ds(q * piece, piece)] = value.astype(out_ref.dtype)

    corners = [(0, 0), (0, 1), (1, 0), (1, 1)]

    def z_first(q):
        corer[q].wait_recv()
        for j in range(1, nz):
            zz = lax.rem(z + j, nz)
            for g, (xx, yy) in enumerate(corners):
                plane_out[q, (j - 1) * 4 + g] = (
                    total[q, block(c, xx, yy, zz)] + core_in[q, block(0, xx, yy, zz)].astype(f32)
                ).astype(bf16)
            slots = pl.ds((j - 1) * 4, 4)
            zr[q, j] = rsend(
                plane_out.at[q, slots], plane_in.at[q, slots], q, 3 + j, z_peer(j)
            )
        for xx, yy in corners:
            total[q, block(c, xx, yy, z)] += core_in[q, block(0, xx, yy, z)].astype(f32)

    def z_then_plane(q):
        for j in range(1, nz):
            zr[q, j].wait_recv()
        for g, (xx, yy) in enumerate(corners):
            value = total[q, block(c, xx, yy, z)]
            for j in range(1, nz):
                value = value + plane_in[q, (j - 1) * 4 + g].astype(f32)
            total[q, block(c, xx, yy, z)] = value
        for p, (xx, yy) in enumerate(plane_at):
            z_out[q, p] = total[q, block(c, xx, yy, z)].astype(bf16)
            planer[q, p] = rsend(z_out.at[q, p], z_in.at[q, p], q, 1 + p, plane_peers[p])

    def z_first_finish(q):
        value = total[q, own]
        for p in range(3):
            planer[q, p].wait_recv()
            value = value + z_in[q, p].astype(f32)
        out_ref[:, pl.ds(q * piece, piece)] = value.astype(out_ref.dtype)

    for q in range(PIECES):
        produce(q)
        if q == 1:
            z_first(0)
        elif q:
            after_core(q - 1)
    after_core(PIECES - 1)
    after_plane(1)
    z_then_plane(0)
    for q in range(2, PIECES):
        after_plane(q)
    finish(1)
    z_first_finish(0)
    for q in range(2, PIECES):
        finish(q)
    for copy in rsends:
        copy.wait_send()


def fused(nz, tokens, expert_ids, gate_values, slot_ids, up_weight, down_weight):
    tok, model = tokens.shape
    per_node, _, width = up_weight.shape
    blocks = 8 * nz
    piece = model // PIECES
    bf16, f32 = jnp.bfloat16, jnp.float32
    vmem = pl.BlockSpec(memory_space=pltpu.VMEM)
    anyspace = pl.BlockSpec(memory_space=pl.ANY)
    dma = pltpu.SemaphoreType.DMA

    def pieces(n):
        return pltpu.VMEM((PIECES, n, tok, piece), bf16)

    return pl.pallas_call(
        functools.partial(fused_kernel, nz),
        out_shape=jax.ShapeDtypeStruct((tok, model), bf16),
        in_specs=[anyspace, vmem, vmem, anyspace, anyspace],
        out_specs=vmem,
        scratch_shapes=[
            pltpu.VMEM(up_weight.shape, bf16),
            pltpu.VMEM(down_weight.shape, bf16),
            pltpu.VMEM((blocks, tok, model + LANES), bf16),
            pltpu.VMEM((blocks * tok, model), bf16),
            pltpu.VMEM((per_node, blocks * tok, width), bf16),
            pltpu.VMEM((PIECES, blocks, tok, piece), f32),
            pieces(4 * nz), pieces(4 * nz),
            pieces(3 * nz), pieces(3 * nz),
            pieces(nz - 1), pieces(nz - 1),
            dma, dma((per_node,)), dma((per_node,)),
            dma((nz - 1,)), dma((nz - 1,)),
            dma((3,)), dma((3,)),
            dma((3, nz)), dma((3, nz)),
            dma((4, nz - 1)), dma((4, nz - 1)),
            dma((4,)), dma((4,)),
            dma((PIECES, 3 + nz)), dma((PIECES, 3 + nz)),
        ],
        compiler_params=pltpu.CompilerParams(
            collective_id=0, has_side_effects=True, vmem_limit_bytes=60 * 1024 * 1024
        ),
    )(tokens, expert_ids, gate_values, up_weight, down_weight)


def body_for(mesh):
    nodes, chips = mesh.shape["node"], mesh.shape["chip"]
    nz = nodes // 4

    def body(tokens, expert_ids, gate_values, slot_ids, up_weight, down_weight):
        tok, model = tokens.shape
        experts = nodes * up_weight.shape[0]
        if (
            chips == 2
            and nodes == 4 * nz
            and nz == 4
            and tok == 8
            and model % (PIECES * LANES) == 0
            and experts <= LANES
        ):
            return fused(nz, tokens, expert_ids, gate_values, slot_ids, up_weight, down_weight)
        return shards(tokens, expert_ids, gate_values, slot_ids, up_weight, down_weight)

    return body


def solution(mesh):
    return jax.shard_map(
        body_for(mesh),
        mesh=mesh,
        in_specs=(
            P(("node", "chip"), None),
            P(("node", "chip"), None),
            P(("node", "chip"), None),
            P(("node", "chip"), None),
            P("node", None, "chip"),
            P("node", "chip", None),
        ),
        out_specs=P(("node", "chip"), None),
        check_vma=False,
    )
```
